32 devices in a mesh: chan: 8 (over y, x, core), win: 4 (over z).
Axes of the slice: x: 2, y: 2, z: 4, core: 2. Of those that a mesh axis runs over, the one named last changes fastest.
Arguments:
- strain: bfloat16 [4096, 4096], P('chan', 'win'), may hold values from -6 to 6
- alive_flags: int32 [4096], P('chan'), may hold values 0 or 1
Outputs:
- correlation: float32 [4096, 2, 4096], P('win', None, 'chan')
The draws below stay inside these ranges and needn't reach their ends.
All inputs are finite; a program needn't handle non-finite values. No bound on the sum of `alive_flags` on one device may be relied on, other than what follows from the above.
Results may differ from the reference program's by a relative error of at most 0.0059.
Values may be sent and summed in bfloat16 or wider, within the bound.
No kernel may reach another device: no remote copies, remote signals or barrier semaphores. Data moves between devices by JAX's collectives and lax.ppermute only.
A program may use at most 128 MiB of HBM per device.

```python
import math
import jax
import jax.numpy as jnp
from jax import lax

CHANNELS = 4096
NF = 256
FIRST_BIN = 64
SEG = 1024
TREND_REACH = 8
LEVEL_REACH = 32
BIN_REACH = 4
LAGS = 2
SEGMENTS = 4
TIME = 4096
N_CHAN = 8


def touch_ends(result, stream_key, smallest, high):
    index_at = [jax.random.randint(jax.random.fold_in(stream_key, axis), (), 0, length) for axis, length in enumerate(result.shape)]
    longest = result.shape.index(max(result.shape))
    neighbour = index_at[:longest] + [(index_at[longest] + 1) % result.shape[longest]] + index_at[longest + 1:]
    return result.at[tuple(index_at)].set(smallest).at[tuple(neighbour)].set(high)


def levels(key, shape, shards, smallest, largest):
    def one(axis_at, parts):
        heights = jax.random.uniform(jax.random.fold_in(jax.random.fold_in(key, 6), axis_at), (parts,), jnp.float32, smallest / len(shards), largest / len(shards))
        return jnp.repeat(jnp.exp(heights), shape[axis_at] // parts).reshape((-1,) + (1,) * (len(shape) - axis_at - 1))

    factor_of = one(*shards[0])
    for cut in shards[1:]:
        factor_of = factor_of * one(*cut)
    return factor_of


def gaussian(rng, shape, scale, bound, split=(), kind=jnp.bfloat16):
    level = levels(rng, shape, split, -0.22, 0.18) if split else 1.0
    entries = jax.random.normal(rng, shape, jnp.float32) * scale * level
    return jnp.minimum(jnp.maximum(entries, -bound), bound).astype(kind)


def setup_inputs(seed: int = 0) -> dict:
    arg_keys = jax.random.split(jax.random.key(seed), 3)
    strain = gaussian(arg_keys[0], (CHANNELS, TIME), 1.0, 6.0, ((0, 8), (1, 4)))
    alive_flags = touch_ends((jax.random.randint(arg_keys[1], (CHANNELS,), 0, 8) < 7).astype(jnp.int32), jax.random.fold_in(arg_keys[1], 1), 0, 1)
    return {"strain": strain, "alive_flags": alive_flags}


def window_sum(values, window_len):
    window_dims = (1,) * (values.ndim - 1) + (window_len,)
    return lax.reduce_window(values, jnp.zeros((), values.dtype), lax.add, window_dims, (1,) * values.ndim, 'VALID')

def condition(padded, trend_reach, level_reach):
    padded_len = padded.shape[-1]
    trend_mean = window_sum(padded, 2 * trend_reach + 1) / (2 * trend_reach + 1)
    detrended = padded[:, trend_reach:padded_len - trend_reach] - trend_mean
    inner_len = detrended.shape[-1]
    level_mean = window_sum(jnp.abs(detrended), 2 * level_reach + 1) / (2 * level_reach + 1)
    return detrended[:, level_reach:inner_len - level_reach] / (level_mean + 1e-05)

def dft_table(seg_len, bin_count, first_bin):
    sample_idx = jnp.arange(seg_len, dtype=jnp.int32)[:, None]
    bin_idx = jnp.arange(bin_count, dtype=jnp.int32)[None, :] + first_bin
    phase_angle = 2.0 * math.pi / seg_len * (sample_idx * bin_idx % seg_len).astype(jnp.float32)
    return jnp.concatenate([jnp.cos(phase_angle), -jnp.sin(phase_angle)], axis=1).astype(jnp.bfloat16)

def lag_tables(seg_len, bin_count, first_bin, lag_count):
    lag_idx = jnp.arange(lag_count, dtype=jnp.int32)[:, None]
    lag_shift = 2 * (2 * lag_idx - lag_count + 1)
    bin_idx = jnp.arange(bin_count, dtype=jnp.int32)[None, :] + first_bin
    phase_angle = 2.0 * math.pi / seg_len * (bin_idx * lag_shift % seg_len).astype(jnp.float32)
    return (jnp.cos(phase_angle), jnp.sin(phase_angle))

def whiten(spectra, alive_col, bin_count, bin_reach):
    real_part = spectra[..., :bin_count]
    imag_part = spectra[..., bin_count:]
    magnitude = jnp.sqrt(real_part * real_part + imag_part * imag_part)
    pad_spec = ((0, 0),) * (magnitude.ndim - 1) + ((bin_reach, bin_reach),)
    smoothed = window_sum(jnp.pad(magnitude, pad_spec), 2 * bin_reach + 1) / (2 * bin_reach + 1)
    level_mean = lax.optimization_barrier(jnp.mean(magnitude, axis=-1, keepdims=True))
    factor = alive_col / (smoothed + level_mean + 1e-05)
    return jnp.concatenate([real_part * factor, imag_part * factor], axis=-1).astype(jnp.bfloat16)

def rotate(panel, lag_cos, lag_sin, bin_count):
    row_count = panel.shape[0]
    split_parts = panel.astype(jnp.float32).reshape(row_count, -1, 2, bin_count)
    real_part = split_parts[None, :, :, 0, :]
    imag_part = split_parts[None, :, :, 1, :]
    cosine = lag_cos[:, None, None, :]
    sine_part = lag_sin[:, None, None, :]
    turned = jnp.stack([real_part * cosine + imag_part * sine_part, imag_part * cosine - real_part * sine_part], axis=3)
    return turned.reshape(lag_cos.shape[0], row_count, -1).astype(jnp.bfloat16)

def reference(strain, alive_flags):
    margin = TREND_REACH + LEVEL_REACH
    row_count = CHANNELS // N_CHAN
    table = dft_table(SEG, NF, FIRST_BIN).astype(jnp.float32)
    blocks = strain.reshape(N_CHAN, row_count, SEG * SEGMENTS)
    flags = alive_flags.reshape(N_CHAN, row_count)

    def spectra_of(block_item):
        chan_block, chan_flags = block_item
        padded = jnp.pad(chan_block.astype(jnp.float32), ((0, 0), (margin, margin)))
        normal = condition(padded, TREND_REACH, LEVEL_REACH)
        pieces = lax.optimization_barrier(normal.astype(jnp.bfloat16)).astype(jnp.float32)
        spectra = jnp.dot(pieces.reshape(row_count * SEGMENTS, SEG), table, precision=lax.Precision.HIGHEST)
        spectra = spectra.reshape(row_count, SEGMENTS, 2 * NF)
        white = whiten(spectra, chan_flags.astype(jnp.float32)[:, None, None], NF, BIN_REACH)
        return white.reshape(row_count, SEGMENTS * 2 * NF)
    white = lax.map(spectra_of, (blocks, flags)).reshape(CHANNELS, SEGMENTS * 2 * NF)
    white = lax.optimization_barrier(white)
    lag_cos, lag_sin = lag_tables(SEG, NF, FIRST_BIN, LAGS)
    turned = lax.optimization_barrier(rotate(white, lag_cos, lag_sin, NF))
    own_spectra = white.astype(jnp.float32)

    def one_lag(turned_panel):
        return jnp.dot(turned_panel.astype(jnp.float32), own_spectra.T, precision=lax.Precision.HIGHEST)
    lag_planes = lax.map(one_lag, turned)
    stack_scale = 1.0 / math.sqrt(NF * SEGMENTS)
    return jnp.transpose(lag_planes, (1, 0, 2)) * stack_scale
```

```python
import functools
import math

import jax
import jax.numpy as jnp
import numpy as np
from jax import lax
from jax.experimental import pallas as pl
from jax.experimental.pallas import tpu as pltpu
from jax.sharding import PartitionSpec as P

NF = 256
FIRST_BIN = 64
SEG = 1024
TREND_REACH = 8
LEVEL_REACH = 32
BIN_REACH = 4
LAGS = 2
EDGE = 128
WIDE = 256
BF16 = jnp.bfloat16
F32 = jnp.float32


def band(rows, columns, shift, reach):
    gap = np.arange(rows)[:, None] - shift - np.arange(columns)[None, :]
    return jnp.asarray((np.abs(gap) <= reach).astype(np.float32), BF16)


def dft_table():
    phase = np.outer(np.arange(SEG), np.arange(NF) + FIRST_BIN) % SEG
    angle = np.float32(2.0 * math.pi / SEG) * phase.astype(np.float32)
    return jnp.asarray(np.concatenate([np.cos(angle), -np.sin(angle)], axis=1), BF16)


def lag_tables():
    shift = 2 * (2 * np.arange(LAGS)[:, None] - LAGS + 1)
    phase = (np.arange(NF)[None, :] + FIRST_BIN) * shift % SEG
    angle = np.float32(2.0 * math.pi / SEG) * phase.astype(np.float32)
    return jnp.asarray(np.cos(angle), F32), jnp.asarray(np.sin(angle), F32)


def split(value):
    high = value.astype(BF16)
    return high, (value - high.astype(F32)).astype(BF16)


def dot(a, b):
    return jnp.dot(a, b, preferred_element_type=F32)


def spectra_kernel(before, middle, after, alive, trend, level, smooth, table, out, padded, distance_hi, distance_lo):
    padded[:, :EDGE] = before[...]
    padded[:, EDGE : EDGE + SEG] = middle[...]
    padded[:, EDGE + SEG :] = after[...]
    total = SEG + 2 * EDGE
    detrended = []
    for start in range(0, total, WIDE):
        low, high = max(start - EDGE, 0), min(start + WIDE + EDGE, total)
        sums = dot(padded[:, low:high], trend[low - start + EDGE : high - start + EDGE, :])
        centre = padded[:, start : start + WIDE].astype(F32)
        part = centre - sums * (1.0 / (2 * TREND_REACH + 1))
        hi, lo = split(jnp.abs(part))
        distance_hi[:, start : start + WIDE] = hi
        distance_lo[:, start : start + WIDE] = lo
        detrended.append(part)
    spectra = None
    for start in range(0, SEG, WIDE):
        window = slice(start, start + WIDE + 2 * EDGE)
        sums = dot(distance_hi[:, window], level[...]) + dot(distance_lo[:, window], level[...])
        left, right = detrended[start // WIDE], detrended[start // WIDE + 1]
        inner = jnp.concatenate([left[:, EDGE:], right[:, :EDGE]], axis=1)
        normal = inner / (sums * (1.0 / (2 * LEVEL_REACH + 1)) + 1e-05)
        product = dot(normal.astype(BF16), table[start : start + WIDE, :])
        spectra = product if spectra is None else spectra + product
    real, imag = spectra[:, :NF], spectra[:, NF:]
    magnitude = jnp.sqrt(real * real + imag * imag)
    hi, lo = split(magnitude)
    smoothed = (dot(hi, smooth[...]) + dot(lo, smooth[...])) * (1.0 / (2 * BIN_REACH + 1))
    mean = jnp.sum(magnitude, axis=1, keepdims=True) * (1.0 / NF)
    factor = alive[...] / (smoothed + mean + 1e-05)
    out[:, :NF] = (real * factor).astype(BF16)
    out[:, NF:] = (imag * factor).astype(BF16)


def whitened(before, strain, after, alive):
    rows = strain.shape[0]
    block = math.gcd(rows, 128)
    by_row = lambda width: pl.BlockSpec((block, width), lambda i: (i, 0))
    whole = lambda a: pl.BlockSpec(a.shape, lambda i: (0, 0))
    constants = (
        band(WIDE + 2 * EDGE, WIDE, EDGE, TREND_REACH),
        band(WIDE + 2 * EDGE, WIDE, EDGE, LEVEL_REACH),
        band(NF, NF, 0, BIN_REACH),
        dft_table(),
    )
    return pl.pallas_call(
        spectra_kernel,
        out_shape=jax.ShapeDtypeStruct((rows, 2 * NF), BF16),
        grid=(rows // block,),
        in_specs=[by_row(EDGE), by_row(SEG), by_row(EDGE), by_row(1)] + [whole(c) for c in constants],
        out_specs=by_row(2 * NF),
        scratch_shapes=[pltpu.VMEM((block, SEG + 2 * EDGE), BF16)] * 3,
        name="whiten",
    )(before, strain, after, alive, *constants)


def turn_into(turned, own, cos, sin):
    for tile in range(own.shape[0] // EDGE):
        rows = own[tile * EDGE : (tile + 1) * EDGE, :].astype(F32)
        real, imag = rows[:, :NF], rows[:, NF:]
        for lag in range(LAGS):
            at = (tile * LAGS + lag) * EDGE
            c, s = cos[lag : lag + 1, :], sin[lag : lag + 1, :]
            turned[at : at + EDGE, :NF] = (real * c - imag * s).astype(BF16)
            turned[at : at + EDGE, NF:] = (real * s + imag * c).astype(BF16)


def correlate_kernel(slots, has_total, last, scale, *refs):
    refs = list(refs)
    refs.pop(0)
    panels = [(refs.pop(0), refs.pop(0)) for _ in range(slots)]
    owns = [refs.pop(0) for _ in range(slots)]
    cos, sin = refs.pop(0), refs.pop(0)
    total = refs.pop(0) if has_total else None
    out, turned = refs
    step = pl.program_id(0)
    half = pl.num_programs(0) // 2

    @pl.when(step == 0)
    def _():
        for slot in range(slots):
            turn_into(turned.at[slot], owns[slot], cos, sin)

    def product(side):
        value = total[...] if has_total else None
        for slot in range(slots):
            term = lax.dot_general(
                panels[slot][side][...],
                turned[slot],
                (((1,), (1,)), ((), ())),
                preferred_element_type=F32,
            )
            value = term if value is None else value + term
        if not last:
            out[...] = value
            return
        value = value * scale
        for lane in range(value.shape[1] // EDGE):
            out[:, lane, :] = value[:, lane * EDGE : (lane + 1) * EDGE]

    @pl.when(step < half)
    def _():
        product(0)

    @pl.when(step >= half)
    def _():
        product(1)


def correlate(core, mine, other, own, total, last, scale):
    slots = len(own)
    rows, depth = mine[0].shape
    block = math.gcd(rows, 128)
    half = rows // block
    width = own[0].shape[0] * LAGS
    cos, sin = lag_tables()

    def row(i, core):
        side = jnp.where(i < half, core[0], 1 - core[0])
        return side * half + lax.rem(i, half)

    in_specs, args = [], []
    for slot in range(slots):
        in_specs.append(pl.BlockSpec((block, depth), lambda i, c: (jnp.minimum(i, half - 1), 0)))
        in_specs.append(pl.BlockSpec((block, depth), lambda i, c: (jnp.maximum(i - half, 0), 0)))
        args += [mine[slot], other[slot]]
    for piece in [*own, cos, sin]:
        in_specs.append(pl.BlockSpec(piece.shape, lambda i, c: (0, 0)))
        args.append(piece)
    if total is not None:
        in_specs.append(pl.BlockSpec((block, width), lambda i, c: (row(i, c), 0)))
        args.append(total)
    if last:
        out_shape = jax.ShapeDtypeStruct((2 * rows, width // EDGE, EDGE), F32)
        out_spec = pl.BlockSpec((block, width // EDGE, EDGE), lambda i, c: (row(i, c), 0, 0))
    else:
        out_shape = jax.ShapeDtypeStruct((2 * rows, width), F32)
        out_spec = pl.BlockSpec((block, width), lambda i, c: (row(i, c), 0))
    return pl.pallas_call(
        functools.partial(correlate_kernel, slots, total is not None, last, scale),
        out_shape=out_shape,
        grid_spec=pltpu.PrefetchScalarGridSpec(
            num_scalar_prefetch=1,
            grid=(2 * half,),
            in_specs=in_specs,
            out_specs=out_spec,
            scratch_shapes=[pltpu.VMEM((slots, width, depth), BF16)],
        ),
        name="correlate_last" if last else "correlate",
    )(core, *args)


def fold_ring(devices):
    return list(range(0, devices, 2))[::1] + list(range(1, devices, 2))[::-1]


def plane_moves(wins, *hops):
    flip = {0: 0, 1: 2, 2: 1, 3: 3}
    pairs = []
    for win in range(wins):
        for start, end in hops:
            for core in range(2):
                a, b = (start, end) if core == 0 else (flip[start], flip[end])
                pairs.append((((win ^ a) * 2 + core) * wins + win, ((win ^ b) * 2 + core) * wins + win))
    return pairs


def square(white):
    wins, chans = lax.axis_size("win"), lax.axis_size("chan")
    chan, win = lax.axis_index("chan"), lax.axis_index("win")
    core = lax.rem(chan, 2)
    role = lax.bitwise_xor(chan // 2, win)
    first, second = jnp.where(core == 0, 1, 2), jnp.where(core == 0, 2, 1)
    is_source, is_first, is_second, is_far = role == 0, role == first, role == second, role == 3
    ring = fold_ring(wins)
    around = [(ring[i], ring[(i + 1) % wins]) for i in range(wins)]
    both = ("chan", "win")
    move = lambda value, *hops: lax.ppermute(value, both, plane_moves(wins, *hops))
    sibling = lambda value: lax.ppermute(value, "chan", [(i, i ^ 1) for i in range(chans)])

    own = [white]
    for _ in range(wins - 1):
        own.append(lax.ppermute(own[-1], "win", around))
    hop1 = move(own[0], (0, 1))
    hop2 = move(hop1, (1, 3))
    mine = []
    for slot in range(wins - 2):
        mixed = move(jnp.where(is_source, own[slot + 1], hop2), (0, 1), (3, 2))
        mine.append(
            jnp.where(is_source, own[slot], jnp.where(is_first, hop1, jnp.where(is_far, hop2, mixed)))
        )
        hop1 = mixed
        hop2 = move(hop1, (1, 3))
    mixed = move(jnp.where(is_source, own[wins - 1], hop2), (0, 1), (3, 2))
    mine.append(jnp.where(is_source, own[wins - 2], jnp.where(is_first, hop1, jnp.where(is_far, hop2, mixed))))
    rest = move(jnp.where(is_source, own[wins - 1], mixed), (0, 2), (1, 3))
    mine.append(jnp.where(is_source, own[wins - 1], jnp.where(is_first, mixed, rest)))
    other = [sibling(piece) for piece in mine]
    return core, own, mine, other


def from_root(value, axis, source):
    kept = jnp.where(lax.axis_index(axis) == source, value, 0).astype(value.dtype)
    return lax.psum(kept, axis)


def general(white):
    wins, chans = lax.axis_size("win"), lax.axis_size("chan")
    segments = lax.all_gather(white, "win", axis=1, tiled=True)
    per_win = chans // wins
    source = lax.axis_index("win") * per_win
    panel = jnp.concatenate([from_root(segments, "chan", source + i) for i in range(per_win)], axis=0)
    cut = lambda value: [value[:, i * 2 * NF : (i + 1) * 2 * NF] for i in range(wins)]
    half = panel.shape[0] // 2
    return jnp.zeros((), jnp.int32), cut(segments), cut(panel[:half]), cut(panel[half:])


def local(strain, alive_flags):
    wins, chans = lax.axis_size("win"), lax.axis_size("chan")
    up = [(i, i + 1) for i in range(wins - 1)]
    down = [(j, i) for i, j in up]
    before = lax.ppermute(strain[:, SEG - EDGE :], "win", up)
    after = lax.ppermute(strain[:, :EDGE], "win", down)
    white = whitened(before, strain, after, alive_flags.astype(F32)[:, None])
    scale = 1.0 / math.sqrt(NF * wins)
    core, own, mine, other = (square if (chans, wins) == (8, 4) else general)(white)
    core = jnp.reshape(core, (1,)).astype(jnp.int32)
    total = None
    cuts = [0, wins - 1, wins] if wins == 4 else list(range(0, wins + 1, 4))
    for start, end in zip(cuts[:-1], cuts[1:]):
        total = correlate(
            core, mine[start:end], other[start:end], own[start:end], total, end == wins, scale
        )
    rows, lanes, _ = total.shape
    tiles = total.reshape(rows, lanes // LAGS, LAGS, EDGE)
    return jnp.transpose(tiles, (0, 2, 1, 3)).reshape(rows, LAGS, lanes // LAGS * EDGE)


def solution(mesh):
    return jax.shard_map(
        local,
        mesh=mesh,
        in_specs=(P("chan", "win"), P("chan")),
        out_specs=P("win", None, "chan"),
        check_vma=False,
    )
```
